512 devices in a mesh: grp: 16 (over y, z_lo), blk: 32 (over x, z_hi, core).
Axes of the slice: x: 4, y: 4, z: 16 (z_hi: 4, z_lo: 4; z = z_hi * 4 + z_lo), core: 2. Of those that a mesh axis runs over, the one named last changes fastest.
Arguments:
- data: bfloat16 [1024, 65536], P('blk'), may hold values from -8 to 8
- labels: int32 [1024], P('blk'), may hold values from -1 to 1, as said below
- order: int32 [32, 4], P('blk'), may hold values from 0 to 3, each once within a row
- reg_index: int32 [16], P('grp'), parts along dimension 0, may hold values from 0 to 5
Outputs:
- dual: float32 [16384], P(('grp', 'blk')), parts along dimension 0
- margins: float32 [16384], P(('grp', 'blk')), parts along dimension 0
- gap: float32 [16], P('grp'), parts along dimension 0
The draws below stay inside these ranges and needn't reach their ends.
There are 16 independent parts, one for each index of `grp`. The reference program is written for one: setup_inputs(seed, part) draws one part's arguments, and reference() takes and returns one part's arrays. A program takes and returns all parts, laid end to end along the dimension named above; an argument that names none is the same for every part. Nothing has to cross between parts.
Inputs may be any that keep to these rules, and one draw needn't show every extreme that they name: `labels`: each entry is -1 or 1.
All inputs are finite; a program needn't handle non-finite values.
Results may differ from the reference program's by a relative error of at most 0.00055.
Values sent between devices are 32-bit elements; how exact they have to be, the bound alone decides.
A program may use at most 64 MiB of HBM per device.

```python
import math
import jax
import jax.numpy as jnp
from jax import lax

F = 65536
ROWS_DEV = 32
NBLOCKS = 4
ROUNDS = 2
SAMPLES = 1024
N_BLK = 32


def common_labels(key):
    return 2 * jax.random.randint(jax.random.fold_in(key, 7), (SAMPLES,), 0, 2) - 1


def draw_labels(key, part):
    return common_labels(key).astype(jnp.int32)


def draw_data(key, part):
    label_signs = common_labels(key).astype(jnp.float32)
    row_index = jnp.arange(SAMPLES, dtype=jnp.int32)
    groups = row_index * 8 // SAMPLES
    one_hot = (groups[:, None] == jnp.arange(8, dtype=jnp.int32)[None, :]).astype(jnp.float32)
    shared_directions = jax.random.normal(jax.random.fold_in(key, 11), (64, F), jnp.float32)
    noise = jax.random.normal(jax.random.fold_in(key, 8), (SAMPLES, F), jnp.float32)
    directions = jax.random.normal(jax.random.fold_in(key, 9), (8, F), jnp.float32)
    loadings = jax.random.normal(jax.random.fold_in(key, 12), (SAMPLES, 64), jnp.float32)
    signal = jnp.dot(one_hot, directions, precision=lax.Precision.HIGHEST)
    shared = math.sqrt(1.5 / 64.0) * jnp.dot(loadings, shared_directions, precision=lax.Precision.HIGHEST)
    values = noise + 0.5 * label_signs[:, None] * signal + shared
    return jnp.clip(values, -8.0, 8.0).astype(jnp.bfloat16)


def setup_inputs(seed: int = 0, part: int = 0) -> dict:
    key_list = jax.random.split(jax.random.key(seed), 5)
    part_splits = jax.random.split(jax.random.fold_in(key_list[4], part), 5)
    data = draw_data(jax.random.fold_in(key_list[4], 71), part)
    labels = draw_labels(jax.random.fold_in(key_list[4], 71), part)
    order = jax.vmap(lambda own: jax.random.permutation(own, NBLOCKS))(jax.random.split(key_list[2], N_BLK)).reshape((N_BLK, NBLOCKS)).astype(jnp.int32)
    reg_index = jax.random.randint(part_splits[3], (1,), 0, 6).astype(jnp.int32)
    return dict(data=data, labels=labels, order=order, reg_index=reg_index)


def local_round(block_data_all, signs, dual, order_row, weights, reg_total, sigma_prime, squared):
    block_rows = block_data_all.shape[0] // NBLOCKS
    feature_scale = 1.0 / math.sqrt(block_data_all.shape[1])
    local_weights = weights
    dual_change = jnp.zeros_like(dual)
    for position in range(NBLOCKS):
        offset = (order_row[position] * block_rows).astype(jnp.int32)
        block_data = lax.dynamic_slice_in_dim(block_data_all, offset, block_rows, 0)
        block_signs = lax.dynamic_slice_in_dim(signs, offset, block_rows, 0)
        block_dual = lax.dynamic_slice_in_dim(dual, offset, block_rows, 0)
        block_change = lax.dynamic_slice_in_dim(dual_change, offset, block_rows, 0)
        block_norms = lax.dynamic_slice_in_dim(squared, offset, block_rows, 0)
        rounded = local_weights.astype(jnp.bfloat16)
        score = feature_scale * jnp.dot(block_data, rounded, preferred_element_type=jnp.float32)
        current = block_dual + block_change
        updated = jnp.clip(current + reg_total * (1.0 - block_signs * score) / (sigma_prime * block_norms), 0.0, 1.0)
        change = updated - current
        dual_change = lax.dynamic_update_slice_in_dim(dual_change, block_change + change, offset, 0)
        coefficient = (block_signs * change).astype(jnp.bfloat16)
        local_weights = local_weights + sigma_prime * feature_scale / reg_total * jnp.dot(coefficient, block_data, preferred_element_type=jnp.float32)
    coefficient = (signs * dual_change).astype(jnp.bfloat16)
    delta = feature_scale / reg_total * jnp.dot(coefficient, block_data_all, preferred_element_type=jnp.float32)
    return (dual_change, delta)

def reference(data, labels, order, reg_index):
    feature_count = data.shape[1]
    feature_scale = 1.0 / math.sqrt(feature_count)
    samples_all = data.shape[0]
    reg_strength = 0.04 * jnp.exp(0.5 * math.log(2.0) * reg_index[0].astype(jnp.float32))
    reg_total = reg_strength * samples_all
    sigma_prime = jnp.float32(N_BLK)
    signs = labels.astype(jnp.float32)
    wide = data.astype(jnp.float32)
    squared = lax.optimization_barrier(jnp.sum(wide * wide, axis=1)) / feature_count + 1e-06
    split_data = data.reshape(N_BLK, ROWS_DEV, feature_count)
    split_signs = signs.reshape(N_BLK, ROWS_DEV)
    split_norms = squared.reshape(N_BLK, ROWS_DEV)
    weights = jnp.zeros((feature_count,), jnp.float32)
    dual = jnp.zeros((N_BLK, ROWS_DEV), jnp.float32)
    mapped = jax.vmap(local_round, in_axes=(0, 0, 0, 0, None, None, None, 0))
    for round_index in range(ROUNDS):
        dual_change, delta = mapped(split_data, split_signs, dual, order, weights, reg_total, sigma_prime, split_norms)
        weights = weights + lax.optimization_barrier(jnp.sum(delta, axis=0))
        dual = dual + dual_change
    dual = dual.reshape(samples_all)
    margins = feature_scale * jnp.dot(data, weights.astype(jnp.bfloat16), preferred_element_type=jnp.float32)
    hinge = jnp.maximum(0.0, 1.0 - signs * margins)
    gap = reg_strength * jnp.sum(weights * weights) + (jnp.sum(hinge) - jnp.sum(dual)) / samples_all
    return (dual, margins, gap.reshape(1))
```

```python
import functools
import math

import jax
import jax.numpy as jnp
from jax import lax
from jax.experimental import pallas as pl
from jax.experimental.pallas import tpu as pltpu
from jax.sharding import PartitionSpec as P

NBLOCKS = 4
ROUNDS = 2
REGS = 6
Y, ZLO = 4, 4
X, ZHI, CORE = 4, 4, 2
PLANE = X * CORE
GRP = Y * ZLO
LANES = 128
MESH = pl.DeviceIdType.MESH


def kernel(
    samples_all,
    chunks,
    labels_ref,
    order_ref,
    reg_ref,
    data_hbm,
    dual_out,
    margins_out,
    gap_out,
    data,
    load_sem,
    delta,
    sums1,
    part2,
    sums2,
    own3,
    weights,
    sums4,
    local5,
    sums5,
    local6,
    sums6,
    plane_send,
    plane_recv,
    cube_send,
    cube_recv,
    grp_send,
    grp_recv,
):
    rows, features = data.shape
    share = features // GRP
    piece = share // PLANE
    grp, blk = lax.axis_index("grp"), lax.axis_index("blk")
    y, zlo = grp // ZLO, lax.rem(grp, ZLO)
    x, zhi, core = blk // (ZHI * CORE), lax.rem(blk // CORE, ZHI), lax.rem(blk, CORE)
    part = lax.rem(zlo + 2 * (zhi // 2), ZLO)
    mine = x * CORE + core

    def plane_peer(d):
        other = lax.rem(mine + d, PLANE)
        return other, (grp, (other // CORE) * ZHI * CORE + zhi * CORE + lax.rem(other, CORE))

    def cube_peer(d):
        other = lax.rem(zhi + d, ZHI)
        other_zlo = lax.rem(part + 2 * (other // 2), ZLO)
        return (y * ZLO + other_zlo, x * ZHI * CORE + other * CORE + core)

    def grp_peer(d):
        return (lax.rem(grp + d, GRP), blk)

    peers = [plane_peer(d)[1] for d in range(1, PLANE)]
    peers += [cube_peer(d) for d in range(1, ZHI)]
    peers += [grp_peer(d) for d in range(1, GRP)]

    width = features // chunks
    loads = [
        pltpu.make_async_copy(
            data_hbm.at[:, pl.ds(i * width, width)],
            data.at[:, pl.ds(i * width, width)],
            load_sem.at[i],
        )
        for i in range(chunks)
    ]
    for load in loads:
        load.start()
    barrier = pltpu.get_barrier_semaphore()
    for peer in peers:
        pl.semaphore_signal(barrier, inc=1, device_id=peer, device_id_type=MESH)

    contract_last = (((1,), (1,)), ((), ()))
    gram = jnp.zeros((rows, rows), jnp.float32)
    for i, load in enumerate(loads):
        load.wait()
        block = data[:, pl.ds(i * width, width)]
        gram = gram + lax.dot_general(
            block, block, contract_last, preferred_element_type=jnp.float32
        )

    scale = 1.0 / math.sqrt(features)
    sigma = float(X * ZHI * CORE)
    reg_row = lax.broadcasted_iota(jnp.int32, (REGS, 1), 0)
    strength = 0.04 * jnp.exp(0.5 * math.log(2.0) * reg_row.astype(jnp.float32))
    total = strength * samples_all
    row = lax.broadcasted_iota(jnp.int32, (rows, rows), 0)
    col = lax.broadcasted_iota(jnp.int32, (rows, rows), 1)
    squared = jnp.sum(jnp.where(row == col, gram, 0.0), axis=0, keepdims=True) / features + 1e-6
    high = gram.astype(jnp.bfloat16)
    low = (gram - high.astype(jnp.float32)).astype(jnp.bfloat16)
    signs = labels_ref[...].astype(jnp.float32)
    block_of = lax.broadcasted_iota(jnp.int32, (1, rows), 1) // (rows // NBLOCKS)
    visits = [block_of == order_ref[0, t] for t in range(NBLOCKS)]
    gain = total / (sigma * squared)
    coupling = sigma * scale * scale / total

    def local_round(base, dual):
        full = jnp.zeros((REGS, rows), jnp.float32)
        new_dual = dual
        for t in range(NBLOCKS):
            score = base
            if t:
                coef = full.astype(jnp.bfloat16)
                score = base + coupling * (
                    jnp.dot(coef, high, preferred_element_type=jnp.float32)
                    + jnp.dot(coef, low, preferred_element_type=jnp.float32)
                )
            updated = jnp.clip(dual + gain * (1.0 - signs * score), 0.0, 1.0)
            step = (signs * (updated - dual)).astype(jnp.bfloat16).astype(jnp.float32)
            full = jnp.where(visits[t], step, full)
            new_dual = jnp.where(visits[t], updated, new_dual)
        return full, new_dual

    dual = jnp.zeros((REGS, rows), jnp.float32)
    full, dual = local_round(jnp.zeros((REGS, rows), jnp.float32), dual)
    pl.semaphore_wait(barrier, len(peers))

    def copy(source, target, sends, recvs, i, peer):
        return pltpu.make_async_remote_copy(
            src_ref=source,
            dst_ref=target,
            send_sem=sends.at[i],
            recv_sem=recvs.at[i],
            device_id=peer,
            device_id_type=MESH,
        )

    pending = []

    def to_plane(stage, make):
        copies = []
        for d in range(1, PLANE):
            other, peer = plane_peer(d)
            source, target = make(d, other)
            c = copy(source, target, plane_send, plane_recv, stage * (PLANE - 1) + d - 1, peer)
            c.start()
            copies.append(c)
        pending.extend(copies)
        return copies

    def to_cubes(stage, source, target):
        copies = []
        for d in range(1, ZHI):
            c = copy(source, target, cube_send, cube_recv, stage * (ZHI - 1) + d - 1, cube_peer(d))
            c.start()
            copies.append(c)
        pending.extend(copies)
        return copies

    def to_grp(stage, source, target):
        copies = []
        for d in range(1, GRP):
            c = copy(source, target, grp_send, grp_recv, stage * (GRP - 1) + d - 1, grp_peer(d))
            c.start()
            copies.append(c)
        pending.extend(copies)
        return copies

    def arrived(copies):
        for c in copies:
            c.wait_recv()

    start = pl.multiple_of((y * ZLO + part) * share, share)
    own = pl.ds(pl.multiple_of(mine * piece, piece), piece)
    held = None
    for r in range(ROUNDS):
        delta[r] = (scale / total) * jnp.dot(
            full.astype(jnp.bfloat16),
            data[:, pl.ds(start, share)],
            preferred_element_type=jnp.float32,
        )

        def scatter(d, other):
            where = pl.ds(pl.multiple_of(other * piece, piece), piece)
            return delta.at[r, :, where], sums1.at[r, d - 1]

        arrived(to_plane(2 * r, scatter))
        summed = delta[r, :, own]
        for d in range(1, PLANE):
            summed = summed + sums1[r, d - 1]

        part2[r] = summed
        sums2[r, zhi] = summed
        arrived(to_cubes(r, part2.at[r], sums2.at[r, zhi]))
        summed = sums2[r, 0]
        for h in range(1, ZHI):
            summed = summed + sums2[r, h]
        held = summed if held is None else held + summed

        own3[r] = held
        weights[r, mine] = held
        arrived(to_plane(2 * r + 1, lambda d, other: (own3.at[r], weights.at[r, mine])))
        score = jnp.zeros((REGS, rows), jnp.float32)
        norm = jnp.zeros((REGS, 1), jnp.float32)
        for j in range(PLANE):
            w = weights[r, j]
            score = score + lax.dot_general(
                w.astype(jnp.bfloat16),
                data[:, pl.ds(pl.multiple_of(start + j * piece, piece), piece)],
                contract_last,
                preferred_element_type=jnp.float32,
            )
            norm = norm + jnp.sum(w * w, axis=1, keepdims=True)
        tile = jnp.concatenate(
            [scale * score, jnp.broadcast_to(norm, (REGS, LANES - rows))], axis=1
        )

        own4 = local5.at[r]
        own4[...] = tile
        sums4[r, grp] = tile
        arrived(to_grp(r, own4, sums4.at[r, grp]))
        tile = sums4[r, 0]
        for j in range(1, GRP):
            tile = tile + sums4[r, j]
        margins, norm = tile[:, :rows], tile[:, rows : rows + 1]
        if r + 1 < ROUNDS:
            full, dual = local_round(margins, dual)

    chosen = reg_row == reg_ref[0]
    dual_out[...] = jnp.sum(jnp.where(chosen, dual, 0.0), axis=0, keepdims=True)
    margins_out[...] = jnp.sum(jnp.where(chosen, margins, 0.0), axis=0, keepdims=True)
    hinge = jnp.maximum(0.0, 1.0 - signs * margins)
    mine_total = jnp.broadcast_to(
        jnp.sum(hinge - dual, axis=1, keepdims=True), (REGS, LANES)
    )
    local6[0] = mine_total
    sums5[mine] = mine_total
    arrived(to_plane(2 * ROUNDS, lambda d, other: (local6.at[0], sums5.at[mine])))
    plane_total = sums5[0]
    for j in range(1, PLANE):
        plane_total = plane_total + sums5[j]
    local6[1] = plane_total
    sums6[zhi] = plane_total
    arrived(to_cubes(ROUNDS, local6.at[1], sums6.at[zhi]))
    all_total = sums6[0]
    for h in range(1, ZHI):
        all_total = all_total + sums6[h]
    gap = strength * norm + all_total[:, :1] / samples_all
    gap_out[...] = jnp.sum(jnp.where(chosen, gap, 0.0), axis=0, keepdims=True)
    for c in pending:
        c.wait_send()


def shards(data, labels, order, reg_index):
    rows, features = data.shape
    share = features // GRP
    piece = share // PLANE
    chunks = 8
    f32 = functools.partial(jax.ShapeDtypeStruct, dtype=jnp.float32)
    vmem = pl.BlockSpec(memory_space=pltpu.VMEM)
    smem = pl.BlockSpec(memory_space=pltpu.SMEM)
    scratch = lambda *shape: pltpu.VMEM(shape, jnp.float32)
    sems = lambda n: pltpu.SemaphoreType.DMA((n,))
    dual, margins, gap = pl.pallas_call(
        functools.partial(kernel, rows * lax.axis_size("blk"), chunks),
        out_shape=(f32((1, rows)), f32((1, rows)), f32((1, 1))),
        in_specs=[vmem, smem, smem, pl.BlockSpec(memory_space=pl.ANY)],
        out_specs=(vmem, vmem, vmem),
        scratch_shapes=[
            pltpu.VMEM((rows, features), jnp.bfloat16),
            sems(chunks),
            scratch(ROUNDS, REGS, share),
            scratch(ROUNDS, PLANE - 1, REGS, piece),
            scratch(ROUNDS, REGS, piece),
            scratch(ROUNDS, ZHI, REGS, piece),
            scratch(ROUNDS, REGS, piece),
            scratch(ROUNDS, PLANE, REGS, piece),
            scratch(ROUNDS, GRP, REGS, LANES),
            scratch(ROUNDS, REGS, LANES),
            scratch(PLANE, REGS, LANES),
            scratch(2, REGS, LANES),
            scratch(ZHI, REGS, LANES),
            sems((2 * ROUNDS + 1) * (PLANE - 1)),
            sems((2 * ROUNDS + 1) * (PLANE - 1)),
            sems((ROUNDS + 1) * (ZHI - 1)),
            sems((ROUNDS + 1) * (ZHI - 1)),
            sems(ROUNDS * (GRP - 1)),
            sems(ROUNDS * (GRP - 1)),
        ],
        compiler_params=pltpu.CompilerParams(collective_id=0, has_side_effects=True),
    )(labels.reshape(1, rows), order, reg_index, data)
    return dual.reshape(rows), margins.reshape(rows), gap.reshape(1)


def solution(mesh):
    placed = (P("blk", None), P("blk"), P("blk", None), P("grp"))
    return jax.shard_map(
        shards,
        mesh=mesh,
        in_specs=placed,
        out_specs=(P(("grp", "blk")), P(("grp", "blk")), P("grp")),
        check_vma=False,
    )
```

```python
import functools
import math

import jax
import jax.numpy as jnp
from jax import lax
from jax.experimental import pallas as pl
from jax.experimental.pallas import tpu as pltpu
from jax.sharding import PartitionSpec as P

NBLOCKS = 4
ROUNDS = 2
REGS = 6
Y, ZLO = 4, 4
X, ZHI, CORE = 4, 4, 2
PLANE = X * CORE
GRP = Y * ZLO
LANES = 128
REACH = 6
MESH = pl.DeviceIdType.MESH


def kernel(
    samples_all,
    chunks,
    labels_hbm,
    order_hbm,
    reg_hbm,
    data_hbm,
    out,
    labels_ref,
    order_ref,
    reg_ref,
    small_sem,
    data,
    load_sem,
    delta,
    sums1,
    part2,
    sums2,
    wide,
    across,
    facts_own,
    facts,
    local3,
    sums3,
    local4,
    sums4,
    last3,
    last_sums3,
    last4,
    last_sums4,
    local5,
    sums5,
    plane_send,
    plane_recv,
    cube_send,
    cube_recv,
    grp_send,
    grp_recv,
    relay,
):
    rows, features = data.shape
    share = features // GRP
    piece = share // PLANE
    wide_rows = PLANE * rows
    grp, blk = lax.axis_index("grp"), lax.axis_index("blk")
    y, zlo = grp // ZLO, lax.rem(grp, ZLO)
    x, zhi, core = blk // (ZHI * CORE), lax.rem(blk // CORE, ZHI), lax.rem(blk, CORE)
    part = lax.rem(zlo + 2 * (zhi // 2), ZLO)
    mine = x * CORE + core

    def plane_peer(d):
        other = lax.rem(mine + d, PLANE)
        return other, (grp, (other // CORE) * ZHI * CORE + zhi * CORE + lax.rem(other, CORE))

    def cube_peer(d):
        other = lax.rem(zhi + d, ZHI)
        other_zlo = lax.rem(part + 2 * (other // 2), ZLO)
        return (y * ZLO + other_zlo, x * ZHI * CORE + other * CORE + core)

    def grp_peer(d):
        return (lax.rem(grp + d, GRP), blk)

    def z_peer(d):
        z = lax.rem(zhi * ZLO + zlo + d + ZHI * ZLO, ZHI * ZLO)
        return (y * ZLO + lax.rem(z, ZLO), x * ZHI * CORE + (z // ZLO) * CORE + core)

    left, right = z_peer(-1), z_peer(1)
    peers = [plane_peer(d)[1] for d in range(1, PLANE)]
    peers += [(lax.rem(grp + d * ZLO, GRP), blk) for d in range(1, Y)]
    peers += [left, right]

    width = features // chunks
    loads = [
        pltpu.make_async_copy(
            data_hbm.at[:, pl.ds(i * width, width)],
            data.at[:, pl.ds(i * width, width)],
            load_sem.at[i],
        )
        for i in range(chunks)
    ]
    for load in loads:
        load.start()
    small = [
        pltpu.make_async_copy(source, target, small_sem.at[i])
        for i, (source, target) in enumerate(
            [(labels_hbm, labels_ref), (order_hbm, order_ref), (reg_hbm, reg_ref)]
        )
    ]
    for load in small:
        load.start()
    barrier = pltpu.get_barrier_semaphore()
    for peer in peers:
        pl.semaphore_signal(barrier, inc=1, device_id=peer, device_id_type=MESH)

    contract_last = (((1,), (1,)), ((), ()))
    gram = jnp.zeros((rows, rows), jnp.float32)
    for i, load in enumerate(loads):
        load.wait()
        block = data[:, pl.ds(i * width, width)]
        gram = gram + lax.dot_general(
            block, block, contract_last, preferred_element_type=jnp.float32
        )

    scale = 1.0 / math.sqrt(features)
    sigma = float(X * ZHI * CORE)
    reg_row = lax.broadcasted_iota(jnp.int32, (REGS, 1), 0)
    strength = 0.04 * jnp.exp(0.5 * math.log(2.0) * reg_row.astype(jnp.float32))
    total = strength * samples_all
    coupling = sigma * scale * scale / total

    def local_round(gram, signs, visit):
        n = gram.shape[0]
        row = lax.broadcasted_iota(jnp.int32, (n, n), 0)
        col = lax.broadcasted_iota(jnp.int32, (n, n), 1)
        diagonal = jnp.sum(jnp.where(row == col, gram, 0.0), axis=0, keepdims=True)
        gain = total / (sigma * (diagonal / features + 1e-6))
        high = gram.astype(jnp.bfloat16)
        low = (gram - high.astype(jnp.float32)).astype(jnp.bfloat16)

        def run(base, dual):
            full = jnp.zeros((REGS, n), jnp.float32)
            new_dual = dual
            for t in range(NBLOCKS):
                score = base
                if t:
                    coef = full.astype(jnp.bfloat16)
                    score = base + coupling * (
                        jnp.dot(coef, high, preferred_element_type=jnp.float32)
                        + jnp.dot(coef, low, preferred_element_type=jnp.float32)
                    )
                updated = jnp.clip(dual + gain * (1.0 - signs * score), 0.0, 1.0)
                step = (signs * (updated - dual)).astype(jnp.bfloat16).astype(jnp.float32)
                full = jnp.where(visit == t, step, full)
                new_dual = jnp.where(visit == t, updated, new_dual)
            return full, new_dual

        return run

    for load in small:
        load.wait()
    signs = labels_ref[...].astype(jnp.float32)
    block_of = lax.broadcasted_iota(jnp.int32, (1, rows), 1) // (rows // NBLOCKS)
    visit = jnp.zeros((1, rows), jnp.int32)
    for t in range(1, NBLOCKS):
        visit = jnp.where(block_of == order_ref[0, t], t, visit)
    zero = jnp.zeros((REGS, rows), jnp.float32)
    full, dual = local_round(gram, signs, visit)(zero, zero)

    slot = y * ZLO + part
    start = pl.multiple_of(slot * share, share)
    own = pl.ds(pl.multiple_of(mine * piece, piece), piece)
    pl.semaphore_wait(barrier, len(peers))

    def copy(source, target, sends, recvs, i, peer):
        return pltpu.make_async_remote_copy(
            src_ref=source,
            dst_ref=target,
            send_sem=sends.at[i],
            recv_sem=recvs.at[i],
            device_id=peer,
            device_id_type=MESH,
        )

    pending = []

    def to_plane(stage, make):
        copies = []
        for d in range(1, PLANE):
            other, peer = plane_peer(d)
            source, target = make(d, other)
            c = copy(source, target, plane_send, plane_recv, stage * (PLANE - 1) + d - 1, peer)
            c.start()
            copies.append(c)
        pending.extend(copies)
        return copies

    def to_cubes(stage, source, target):
        copies = []
        for d in range(1, ZHI):
            c = copy(source, target, cube_send, cube_recv, stage * (ZHI - 1) + d - 1, cube_peer(d))
            c.start()
            copies.append(c)
        pending.extend(copies)
        return copies

    def to_grp(stage, source, target):
        copies = []
        for d in range(1, GRP):
            c = copy(source, target, grp_send, grp_recv, stage * (GRP - 1) + d - 1, grp_peer(d))
            c.start()
            copies.append(c)
        pending.extend(copies)
        return copies

    def arrived(copies):
        for c in copies:
            c.wait_recv()

    def summed(ref, count):
        out = ref[0]
        for j in range(1, count):
            out = out + ref[j]
        return out

    delta[...] = (scale / total) * jnp.dot(
        full.astype(jnp.bfloat16), data[:, pl.ds(start, share)], preferred_element_type=jnp.float32
    )

    def scatter(d, other):
        where = pl.ds(pl.multiple_of(other * piece, piece), piece)
        return delta.at[:, where], sums1.at[d - 1]

    scattered = to_plane(0, scatter)
    for j in range(PLANE):
        where = pl.ds(pl.multiple_of(start + j * piece, piece), piece)
        wide[j] = data[:, where].astype(jnp.float32)

    per_half = LANES // rows
    lane = lax.broadcasted_iota(jnp.int32, (1, LANES), 1) // rows
    known = jnp.concatenate([signs, visit.astype(jnp.float32), dual], axis=0)
    known = jnp.concatenate([known] * per_half, axis=1)
    known = jnp.where(lane == lax.rem(mine, per_half), known, 0.0)
    packed = jnp.concatenate([gram[8 * i : 8 * i + 8] for i in range(per_half)], axis=1)
    known = jnp.concatenate([packed, known], axis=0)
    facts_own[...] = known
    facts[mine] = known
    across[mine] = data[:, pl.ds(pl.multiple_of(start + mine * piece, piece), piece)].astype(
        jnp.float32
    )

    notes = to_plane(1, lambda d, other: (facts_own, facts.at[mine]))
    pieces = to_plane(2, lambda d, other: (wide.at[other], across.at[mine]))

    for s in range(REACH - 1):
        pl.semaphore_signal(relay.at[0, s], inc=1, device_id=right, device_id_type=MESH)
        pl.semaphore_signal(relay.at[1, s], inc=1, device_id=left, device_id_type=MESH)
        pl.semaphore_wait(relay.at[0, s], 1)
        pl.semaphore_wait(relay.at[1, s], 1)

    arrived(scattered)
    step = delta[:, own] + summed(sums1, PLANE - 1)

    held = None
    for r in range(ROUNDS):
        part2[r] = step
        sums2[r, zhi] = step
        cubes = to_cubes(r, part2.at[r], sums2.at[r, zhi])
        if r == 0:
            arrived(notes)
            half = PLANE // 2
            low_half, high_half = facts[0, 8:], facts[half, 8:]
            for j in range(1, half):
                low_half = low_half + facts[j, 8:]
                high_half = high_half + facts[half + j, 8:]
            known = jnp.concatenate([low_half, high_half], axis=1)
            signs, visit, dual = known[0:1], known[1:2].astype(jnp.int32), known[2:]
            gram = []
            for j in range(PLANE):
                packed = facts[j, :8]
                parts = [packed[:, i * rows : (i + 1) * rows] for i in range(per_half)]
                one = [jnp.concatenate(parts, axis=0)]
                if j:
                    one = [jnp.zeros((rows, j * rows), jnp.float32)] + one
                if j + 1 < PLANE:
                    one = one + [jnp.zeros((rows, (PLANE - 1 - j) * rows), jnp.float32)]
                gram.append(jnp.concatenate(one, axis=1))
            gram = jnp.concatenate(gram, axis=0)
            solve = local_round(gram, signs, visit)
            arrived(pieces)
            block = across[...].reshape(wide_rows, piece).astype(jnp.bfloat16)
        arrived(cubes)
        step = summed(sums2.at[r], ZHI)
        held = step if held is None else held + step

        tile = scale * lax.dot_general(
            held.astype(jnp.bfloat16), block, contract_last, preferred_element_type=jnp.float32
        )
        last = r + 1 == ROUNDS
        if last:
            norm = jnp.sum(held * held, axis=1, keepdims=True)
            lanes = lax.broadcasted_iota(jnp.int32, (REGS, wide_rows), 1)
            norm = jnp.sum(jnp.where(lanes == reg_row, norm, 0.0), axis=0, keepdims=True)
            tile = jnp.concatenate([tile, norm], axis=0)
        own3, all3, own4, all4 = (
            (last3, last_sums3, last4, last_sums4) if last else (local3, sums3, local4, sums4)
        )
        own3[...] = tile
        all3[mine] = tile
        arrived(to_plane(3 + r, lambda d, other: (own3, all3.at[mine])))
        tile = summed(all3, PLANE)
        own4[...] = tile
        all4[slot] = tile
        arrived(to_grp(r, own4, all4.at[slot]))
        tile = summed(all4, GRP)
        margins = tile[:REGS]
        if not last:
            full, dual = solve(margins, dual)
            step = (scale / total) * jnp.dot(
                full.astype(jnp.bfloat16), block, preferred_element_type=jnp.float32
            )

    hinge = jnp.maximum(0.0, 1.0 - signs * margins)
    cube_total = jnp.broadcast_to(jnp.sum(hinge - dual, axis=1, keepdims=True), (REGS, LANES))
    local5[...] = cube_total
    sums5[zhi] = cube_total
    cubes = to_cubes(ROUNDS, local5, sums5.at[zhi])

    chosen = reg_row == reg_ref[0, 0]

    def own_rows(values):
        values = jnp.sum(jnp.where(chosen, values, 0.0), axis=0, keepdims=True)
        out = jnp.zeros((1, rows), jnp.float32)
        for j in range(PLANE):
            out = out + jnp.where(mine == j, values[:, j * rows : (j + 1) * rows], 0.0)
        return out

    own_dual, own_margins = own_rows(dual), own_rows(margins)
    norm = jnp.sum(
        jnp.where(lax.broadcasted_iota(jnp.int32, (1, wide_rows), 1) == reg_ref[0, 0], tile[REGS:], 0.0),
        axis=1,
        keepdims=True,
    )
    arrived(cubes)
    everyone = summed(sums5, ZHI)[:, :1]
    gap = jnp.sum(jnp.where(chosen, everyone / samples_all, 0.0), axis=0, keepdims=True)
    gap = gap + norm * jnp.sum(jnp.where(chosen, strength, 0.0), axis=0, keepdims=True)
    rest = LANES - 2 * rows
    out[...] = jnp.concatenate([own_dual, own_margins, jnp.broadcast_to(gap, (1, rest))], axis=1)
    for c in pending:
        c.wait_send()


def shards(data, labels, order, reg_index):
    rows, features = data.shape
    share = features // GRP
    piece = share // PLANE
    chunks = 8
    f32 = functools.partial(jax.ShapeDtypeStruct, dtype=jnp.float32)
    vmem = pl.BlockSpec(memory_space=pltpu.VMEM)
    scratch = lambda *shape: pltpu.VMEM(shape, jnp.float32)
    sems = lambda n: pltpu.SemaphoreType.DMA((n,))
    wide_rows = PLANE * rows
    known = 8 + 2 + REGS
    out = pl.pallas_call(
        functools.partial(kernel, rows * lax.axis_size("blk"), chunks),
        out_shape=f32((1, LANES)),
        in_specs=[pl.BlockSpec(memory_space=pl.ANY)] * 4,
        out_specs=vmem,
        scratch_shapes=[
            pltpu.VMEM((1, rows), jnp.int32),
            pltpu.SMEM((1, NBLOCKS), jnp.int32),
            pltpu.SMEM((1, 1), jnp.int32),
            sems(3),
            pltpu.VMEM((rows, features), jnp.bfloat16),
            sems(chunks),
            scratch(REGS, share),
            scratch(PLANE - 1, REGS, piece),
            scratch(ROUNDS, REGS, piece),
            scratch(ROUNDS, ZHI, REGS, piece),
            scratch(PLANE, rows, piece),
            scratch(PLANE, rows, piece),
            scratch(known, LANES),
            scratch(PLANE, known, LANES),
            scratch(REGS, wide_rows),
            scratch(PLANE, REGS, wide_rows),
            scratch(REGS, wide_rows),
            scratch(GRP, REGS, wide_rows),
            scratch(REGS + 1, wide_rows),
            scratch(PLANE, REGS + 1, wide_rows),
            scratch(REGS + 1, wide_rows),
            scratch(GRP, REGS + 1, wide_rows),
            scratch(REGS, LANES),
            scratch(ZHI, REGS, LANES),
            sems((3 + ROUNDS) * (PLANE - 1)),
            sems((3 + ROUNDS) * (PLANE - 1)),
            sems((ROUNDS + 1) * (ZHI - 1)),
            sems((ROUNDS + 1) * (ZHI - 1)),
            sems(ROUNDS * (GRP - 1)),
            sems(ROUNDS * (GRP - 1)),
            pltpu.SemaphoreType.REGULAR((2, REACH - 1)),
        ],
        compiler_params=pltpu.CompilerParams(collective_id=0, has_side_effects=True),
    )(labels.reshape(1, rows), order, reg_index.reshape(1, 1), data)
    out = out.reshape(LANES)
    return out[:rows], out[rows : 2 * rows], out[2 * rows : 2 * rows + 1]


def solution(mesh):
    placed = (P("blk", None), P("blk"), P("blk", None), P("grp"))
    return jax.shard_map(
        shards,
        mesh=mesh,
        in_specs=placed,
        out_specs=(P(("grp", "blk")), P(("grp", "blk")), P("grp")),
        check_vma=False,
    )
```

```python
import functools
import math

import jax
import jax.numpy as jnp
from jax import lax
from jax.experimental import pallas as pl
from jax.experimental.pallas import tpu as pltpu
from jax.sharding import PartitionSpec as P

NBLOCKS = 4
ROUNDS = 2
REGS = 6
Y, ZLO = 4, 4
X, ZHI, CORE = 4, 4, 2
PLANE = X * CORE
GRP = Y * ZLO
LANES = 128
MESH = pl.DeviceIdType.MESH


def kernel(
    samples_all,
    chunks,
    labels_hbm,
    order_hbm,
    reg_hbm,
    data_hbm,
    out,
    labels_ref,
    order_ref,
    reg_ref,
    small_sem,
    data,
    load_sem,
    delta,
    sums1,
    part2,
    sums2,
    wide,
    across,
    facts_own,
    facts,
    local3,
    sums3,
    local4,
    sums4,
    last3,
    last_sums3,
    last4,
    last_sums4,
    local5,
    sums5,
    plane_send,
    plane_recv,
    cube_send,
    cube_recv,
    grp_send,
    grp_recv,
):
    rows, features = data.shape
    share = features // GRP
    piece = share // PLANE
    wide_rows = PLANE * rows
    grp, blk = lax.axis_index("grp"), lax.axis_index("blk")
    y, zlo = grp // ZLO, lax.rem(grp, ZLO)
    x, zhi, core = blk // (ZHI * CORE), lax.rem(blk // CORE, ZHI), lax.rem(blk, CORE)
    part = lax.rem(zlo + 2 * (zhi // 2), ZLO)
    mine = x * CORE + core

    def plane_peer(d):
        other = lax.rem(mine + d, PLANE)
        return other, (grp, (other // CORE) * ZHI * CORE + zhi * CORE + lax.rem(other, CORE))

    def cube_peer(d):
        other = lax.rem(zhi + d, ZHI)
        other_zlo = lax.rem(part + 2 * (other // 2), ZLO)
        return (y * ZLO + other_zlo, x * ZHI * CORE + other * CORE + core)

    def grp_peer(d):
        return (lax.rem(grp + d, GRP), blk)

    peers = [cube_peer(d) for d in (2, 1, 3)]
    peers += [grp_peer(d) for d in range(1, GRP)]
    peers += [plane_peer(d)[1] for d in range(1, PLANE)]
    width = features // chunks
    loads = [
        pltpu.make_async_copy(
            data_hbm.at[:, pl.ds(i * width, width)],
            data.at[:, pl.ds(i * width, width)],
            load_sem.at[i],
        )
        for i in range(chunks)
    ]
    for load in loads:
        load.start()
    small = [
        pltpu.make_async_copy(source, target, small_sem.at[i])
        for i, (source, target) in enumerate(
            [(labels_hbm, labels_ref), (order_hbm, order_ref), (reg_hbm, reg_ref)]
        )
    ]
    for load in small:
        load.start()
    barrier = pltpu.get_barrier_semaphore()
    for peer in peers:
        pl.semaphore_signal(barrier, inc=1, device_id=peer, device_id_type=MESH)

    contract_last = (((1,), (1,)), ((), ()))
    gram = jnp.zeros((rows, rows), jnp.float32)
    for i, load in enumerate(loads):
        load.wait()
        block = data[:, pl.ds(i * width, width)]
        gram = gram + lax.dot_general(
            block, block, contract_last, preferred_element_type=jnp.float32
        )

    scale = 1.0 / math.sqrt(features)
    sigma = float(X * ZHI * CORE)
    reg_row = lax.broadcasted_iota(jnp.int32, (REGS, 1), 0)
    strength = 0.04 * jnp.exp(0.5 * math.log(2.0) * reg_row.astype(jnp.float32))
    total = strength * samples_all
    coupling = sigma * scale * scale / total

    def local_round(gram, signs, visit):
        n = gram.shape[0]
        row = lax.broadcasted_iota(jnp.int32, (n, n), 0)
        col = lax.broadcasted_iota(jnp.int32, (n, n), 1)
        diagonal = jnp.sum(jnp.where(row == col, gram, 0.0), axis=0, keepdims=True)
        gain = total / (sigma * (diagonal / features + 1e-6))
        high = gram.astype(jnp.bfloat16)
        low = (gram - high.astype(jnp.float32)).astype(jnp.bfloat16)

        def run(base, dual):
            full = jnp.zeros((REGS, n), jnp.float32)
            new_dual = dual
            for t in range(NBLOCKS):
                score = base
                if t:
                    coef = full.astype(jnp.bfloat16)
                    score = base + coupling * (
                        jnp.dot(coef, high, preferred_element_type=jnp.float32)
                        + jnp.dot(coef, low, preferred_element_type=jnp.float32)
                    )
                updated = jnp.clip(dual + gain * (1.0 - signs * score), 0.0, 1.0)
                step = (signs * (updated - dual)).astype(jnp.bfloat16).astype(jnp.float32)
                full = jnp.where(visit == t, step, full)
                new_dual = jnp.where(visit == t, updated, new_dual)
            return full, new_dual

        return run

    for load in small:
        load.wait()
    signs = labels_ref[...].astype(jnp.float32)
    block_of = lax.broadcasted_iota(jnp.int32, (1, rows), 1) // (rows // NBLOCKS)
    visit = jnp.zeros((1, rows), jnp.int32)
    for t in range(1, NBLOCKS):
        visit = jnp.where(block_of == order_ref[0, t], t, visit)
    zero = jnp.zeros((REGS, rows), jnp.float32)
    full, dual = local_round(gram, signs, visit)(zero, zero)

    slot = y * ZLO + part
    start = pl.multiple_of(slot * share, share)
    own = pl.ds(pl.multiple_of(mine * piece, piece), piece)

    def copy(source, target, sends, recvs, i, peer):
        return pltpu.make_async_remote_copy(
            src_ref=source,
            dst_ref=target,
            send_sem=sends.at[i],
            recv_sem=recvs.at[i],
            device_id=peer,
            device_id_type=MESH,
        )

    pending = []

    def to_plane(stage, make):
        copies = []
        for d in range(1, PLANE):
            other, peer = plane_peer(d)
            source, target = make(d, other)
            c = copy(source, target, plane_send, plane_recv, stage * (PLANE - 1) + d - 1, peer)
            c.start()
            copies.append(c)
        pending.extend(copies)
        return copies

    def to_cubes(stage, source, target):
        copies = []
        for d in range(1, ZHI):
            c = copy(source, target, cube_send, cube_recv, stage * (ZHI - 1) + d - 1, cube_peer(d))
            c.start()
            copies.append(c)
        pending.extend(copies)
        return copies

    def to_grp(stage, source, target):
        copies = []
        for d in range(1, GRP):
            c = copy(source, target, grp_send, grp_recv, stage * (GRP - 1) + d - 1, grp_peer(d))
            c.start()
            copies.append(c)
        pending.extend(copies)
        return copies

    def arrived(copies):
        for c in copies:
            c.wait_recv()

    def summed(ref, count):
        out = ref[0]
        for j in range(1, count):
            out = out + ref[j]
        return out

    delta[...] = (scale / total) * jnp.dot(
        full.astype(jnp.bfloat16), data[:, pl.ds(start, share)], preferred_element_type=jnp.float32
    )

    pl.semaphore_wait(barrier, len(peers))

    def scatter(d, other):
        where = pl.ds(pl.multiple_of(other * piece, piece), piece)
        return delta.at[:, where], sums1.at[d - 1]

    scattered = to_plane(0, scatter)
    for j in range(PLANE):
        where = pl.ds(pl.multiple_of(start + j * piece, piece), piece)
        wide[j] = data[:, where].astype(jnp.float32)

    per_half = LANES // rows
    lane = lax.broadcasted_iota(jnp.int32, (1, LANES), 1) // rows
    known = jnp.concatenate([signs, visit.astype(jnp.float32), dual], axis=0)
    known = jnp.concatenate([known] * per_half, axis=1)
    known = jnp.where(lane == lax.rem(mine, per_half), known, 0.0)
    packed = jnp.concatenate([gram[8 * i : 8 * i + 8] for i in range(per_half)], axis=1)
    known = jnp.concatenate([packed, known], axis=0)
    facts_own[...] = known
    facts[mine] = known
    across[mine] = data[:, pl.ds(pl.multiple_of(start + mine * piece, piece), piece)].astype(
        jnp.float32
    )

    notes = to_plane(1, lambda d, other: (facts_own, facts.at[mine]))
    pieces = to_plane(2, lambda d, other: (wide.at[other], across.at[mine]))

    arrived(scattered)
    step = delta[:, own] + summed(sums1, PLANE - 1)

    held = None
    for r in range(ROUNDS):
        part2[r] = step
        sums2[r, zhi] = step
        cubes = to_cubes(r, part2.at[r], sums2.at[r, zhi])
        if r == 0:
            arrived(notes)
            half = PLANE // 2
            low_half, high_half = facts[0, 8:], facts[half, 8:]
            for j in range(1, half):
                low_half = low_half + facts[j, 8:]
                high_half = high_half + facts[half + j, 8:]
            known = jnp.concatenate([low_half, high_half], axis=1)
            signs, visit, dual = known[0:1], known[1:2].astype(jnp.int32), known[2:]
            gram = []
            for j in range(PLANE):
                packed = facts[j, :8]
                parts = [packed[:, i * rows : (i + 1) * rows] for i in range(per_half)]
                one = [jnp.concatenate(parts, axis=0)]
                if j:
                    one = [jnp.zeros((rows, j * rows), jnp.float32)] + one
                if j + 1 < PLANE:
                    one = one + [jnp.zeros((rows, (PLANE - 1 - j) * rows), jnp.float32)]
                gram.append(jnp.concatenate(one, axis=1))
            gram = jnp.concatenate(gram, axis=0)
            solve = local_round(gram, signs, visit)
            arrived(pieces)
            block = across[...].reshape(wide_rows, piece).astype(jnp.bfloat16)
        arrived(cubes)
        step = summed(sums2.at[r], ZHI)
        held = step if held is None else held + step

        tile = scale * lax.dot_general(
            held.astype(jnp.bfloat16), block, contract_last, preferred_element_type=jnp.float32
        )
        last = r + 1 == ROUNDS
        if last:
            norm = jnp.sum(held * held, axis=1, keepdims=True)
            lanes = lax.broadcasted_iota(jnp.int32, (REGS, wide_rows), 1)
            norm = jnp.sum(jnp.where(lanes == reg_row, norm, 0.0), axis=0, keepdims=True)
            tile = jnp.concatenate([tile, norm], axis=0)
        own3, all3, own4, all4 = (
            (last3, last_sums3, last4, last_sums4) if last else (local3, sums3, local4, sums4)
        )
        own3[...] = tile
        all3[mine] = tile
        arrived(to_plane(3 + r, lambda d, other: (own3, all3.at[mine])))
        tile = summed(all3, PLANE)
        own4[...] = tile
        all4[slot] = tile
        arrived(to_grp(r, own4, all4.at[slot]))
        tile = summed(all4, GRP)
        margins = tile[:REGS]
        if not last:
            full, dual = solve(margins, dual)
            step = (scale / total) * jnp.dot(
                full.astype(jnp.bfloat16), block, preferred_element_type=jnp.float32
            )

    hinge = jnp.maximum(0.0, 1.0 - signs * margins)
    cube_total = jnp.broadcast_to(jnp.sum(hinge - dual, axis=1, keepdims=True), (REGS, LANES))
    local5[...] = cube_total
    sums5[zhi] = cube_total
    cubes = to_cubes(ROUNDS, local5, sums5.at[zhi])

    chosen = reg_row == reg_ref[0, 0]

    def own_rows(values):
        values = jnp.sum(jnp.where(chosen, values, 0.0), axis=0, keepdims=True)
        out = jnp.zeros((1, rows), jnp.float32)
        for j in range(PLANE):
            out = out + jnp.where(mine == j, values[:, j * rows : (j + 1) * rows], 0.0)
        return out

    own_dual, own_margins = own_rows(dual), own_rows(margins)
    norm = jnp.sum(
        jnp.where(lax.broadcasted_iota(jnp.int32, (1, wide_rows), 1) == reg_ref[0, 0], tile[REGS:], 0.0),
        axis=1,
        keepdims=True,
    )
    arrived(cubes)
    everyone = summed(sums5, ZHI)[:, :1]
    gap = jnp.sum(jnp.where(chosen, everyone / samples_all, 0.0), axis=0, keepdims=True)
    gap = gap + norm * jnp.sum(jnp.where(chosen, strength, 0.0), axis=0, keepdims=True)
    rest = LANES - 2 * rows
    out[...] = jnp.concatenate([own_dual, own_margins, jnp.broadcast_to(gap, (1, rest))], axis=1)
    for c in pending:
        c.wait_send()


def shards(data, labels, order, reg_index):
    rows, features = data.shape
    share = features // GRP
    piece = share // PLANE
    chunks = 8
    f32 = functools.partial(jax.ShapeDtypeStruct, dtype=jnp.float32)
    vmem = pl.BlockSpec(memory_space=pltpu.VMEM)
    scratch = lambda *shape: pltpu.VMEM(shape, jnp.float32)
    sems = lambda n: pltpu.SemaphoreType.DMA((n,))
    wide_rows = PLANE * rows
    known = 8 + 2 + REGS
    out = pl.pallas_call(
        functools.partial(kernel, rows * lax.axis_size("blk"), chunks),
        out_shape=f32((1, LANES)),
        in_specs=[pl.BlockSpec(memory_space=pl.ANY)] * 4,
        out_specs=vmem,
        scratch_shapes=[
            pltpu.VMEM((1, rows), jnp.int32),
            pltpu.SMEM((1, NBLOCKS), jnp.int32),
            pltpu.SMEM((1, 1), jnp.int32),
            sems(3),
            pltpu.VMEM((rows, features), jnp.bfloat16),
            sems(chunks),
            scratch(REGS, share),
            scratch(PLANE - 1, REGS, piece),
            scratch(ROUNDS, REGS, piece),
            scratch(ROUNDS, ZHI, REGS, piece),
            scratch(PLANE, rows, piece),
            scratch(PLANE, rows, piece),
            scratch(known, LANES),
            scratch(PLANE, known, LANES),
            scratch(REGS, wide_rows),
            scratch(PLANE, REGS, wide_rows),
            scratch(REGS, wide_rows),
            scratch(GRP, REGS, wide_rows),
            scratch(REGS + 1, wide_rows),
            scratch(PLANE, REGS + 1, wide_rows),
            scratch(REGS + 1, wide_rows),
            scratch(GRP, REGS + 1, wide_rows),
            scratch(REGS, LANES),
            scratch(ZHI, REGS, LANES),
            sems((3 + ROUNDS) * (PLANE - 1)),
            sems((3 + ROUNDS) * (PLANE - 1)),
            sems((ROUNDS + 1) * (ZHI - 1)),
            sems((ROUNDS + 1) * (ZHI - 1)),
            sems(ROUNDS * (GRP - 1)),
            sems(ROUNDS * (GRP - 1)),
        ],
        compiler_params=pltpu.CompilerParams(collective_id=0, has_side_effects=True),
    )(labels.reshape(1, rows), order, reg_index.reshape(1, 1), data)
    out = out.reshape(LANES)
    return out[:rows], out[rows : 2 * rows], out[2 * rows : 2 * rows + 1]


def solution(mesh):
    placed = (P("blk", None), P("blk"), P("blk", None), P("grp"))
    return jax.shard_map(
        shards,
        mesh=mesh,
        in_specs=placed,
        out_specs=(P(("grp", "blk")), P(("grp", "blk")), P("grp")),
        check_vma=False,
    )
```

```python
import functools
import math

import jax
import jax.numpy as jnp
from jax import lax
from jax.experimental import pallas as pl
from jax.experimental.pallas import tpu as pltpu
from jax.sharding import PartitionSpec as P

NBLOCKS = 4
ROUNDS = 2
REGS = 6
Y, ZLO = 4, 4
X, ZHI, CORE = 4, 4, 2
PLANE = X * CORE
GRP = Y * ZLO
LANES = 128
MESH = pl.DeviceIdType.MESH


def kernel(
    samples_all,
    chunks,
    labels_hbm,
    order_hbm,
    reg_hbm,
    data_hbm,
    out,
    labels_ref,
    order_ref,
    reg_ref,
    small_sem,
    data,
    load_sem,
    delta,
    sums1,
    part2,
    sums2,
    wide,
    across,
    facts_own,
    facts,
    local3,
    sums3,
    local4,
    sums4,
    last3,
    last_sums3,
    last4,
    last_sums4,
    local5,
    sums5,
    plane_send,
    plane_recv,
    cube_send,
    cube_recv,
    grp_send,
    grp_recv,
):
    rows, features = data.shape
    width = features // chunks
    loads = [
        pltpu.make_async_copy(
            data_hbm.at[:, pl.ds(i * width, width)],
            data.at[:, pl.ds(i * width, width)],
            load_sem.at[i],
        )
        for i in range(chunks)
    ]
    for load in loads:
        load.start()
    small = [
        pltpu.make_async_copy(source, target, small_sem.at[i])
        for i, (source, target) in enumerate(
            [(labels_hbm, labels_ref), (order_hbm, order_ref), (reg_hbm, reg_ref)]
        )
    ]
    for load in small:
        load.start()
    share = features // GRP
    piece = share // PLANE
    wide_rows = PLANE * rows
    grp, blk = lax.axis_index("grp"), lax.axis_index("blk")
    y, zlo = grp // ZLO, lax.rem(grp, ZLO)
    x, zhi, core = blk // (ZHI * CORE), lax.rem(blk // CORE, ZHI), lax.rem(blk, CORE)
    part = lax.rem(zlo + 2 * (zhi // 2), ZLO)
    mine = x * CORE + core

    def plane_peer(d):
        other = lax.rem(mine + d, PLANE)
        return other, (grp, (other // CORE) * ZHI * CORE + zhi * CORE + lax.rem(other, CORE))

    def cube_peer(d):
        other = lax.rem(zhi + d, ZHI)
        other_zlo = lax.rem(part + 2 * (other // 2), ZLO)
        return (y * ZLO + other_zlo, x * ZHI * CORE + other * CORE + core)

    def grp_peer(d):
        return (lax.rem(grp + d, GRP), blk)

    peers = [cube_peer(d) for d in (2, 1, 3)]
    peers += [grp_peer(d) for d in range(1, GRP)]
    peers += [plane_peer(d)[1] for d in range(1, PLANE)]
    barrier = pltpu.get_barrier_semaphore()
    for peer in peers:
        pl.semaphore_signal(barrier, inc=1, device_id=peer, device_id_type=MESH)

    contract_last = (((1,), (1,)), ((), ()))
    gram = jnp.zeros((rows, rows), jnp.float32)
    for i, load in enumerate(loads):
        load.wait()
        block = data[:, pl.ds(i * width, width)]
        gram = gram + lax.dot_general(
            block, block, contract_last, preferred_element_type=jnp.float32
        )

    scale = 1.0 / math.sqrt(features)
    sigma = float(X * ZHI * CORE)
    reg_row = lax.broadcasted_iota(jnp.int32, (REGS, 1), 0)
    strength = 0.04 * jnp.exp(0.5 * math.log(2.0) * reg_row.astype(jnp.float32))
    total = strength * samples_all
    coupling = sigma * scale * scale / total

    def local_round(gram, signs, visit):
        n = gram.shape[0]
        row = lax.broadcasted_iota(jnp.int32, (n, n), 0)
        col = lax.broadcasted_iota(jnp.int32, (n, n), 1)
        diagonal = jnp.sum(jnp.where(row == col, gram, 0.0), axis=0, keepdims=True)
        gain = total / (sigma * (diagonal / features + 1e-6))
        high = gram.astype(jnp.bfloat16)
        low = (gram - high.astype(jnp.float32)).astype(jnp.bfloat16)

        def run(base, dual):
            full = jnp.zeros((REGS, n), jnp.float32)
            new_dual = dual
            for t in range(NBLOCKS):
                score = base
                if t:
                    coef = full.astype(jnp.bfloat16)
                    score = base + coupling * (
                        jnp.dot(coef, high, preferred_element_type=jnp.float32)
                        + jnp.dot(coef, low, preferred_element_type=jnp.float32)
                    )
                updated = jnp.clip(dual + gain * (1.0 - signs * score), 0.0, 1.0)
                step = (signs * (updated - dual)).astype(jnp.bfloat16).astype(jnp.float32)
                full = jnp.where(visit == t, step, full)
                new_dual = jnp.where(visit == t, updated, new_dual)
            return full, new_dual

        return run

    for load in small:
        load.wait()
    signs = labels_ref[...].astype(jnp.float32)
    block_of = lax.broadcasted_iota(jnp.int32, (1, rows), 1) // (rows // NBLOCKS)
    visit = jnp.zeros((1, rows), jnp.int32)
    for t in range(1, NBLOCKS):
        visit = jnp.where(block_of == order_ref[0, t], t, visit)
    zero = jnp.zeros((REGS, rows), jnp.float32)
    full, dual = local_round(gram, signs, visit)(zero, zero)

    slot = y * ZLO + part
    start = pl.multiple_of(slot * share, share)
    own = pl.ds(pl.multiple_of(mine * piece, piece), piece)

    def copy(source, target, sends, recvs, i, peer):
        return pltpu.make_async_remote_copy(
            src_ref=source,
            dst_ref=target,
            send_sem=sends.at[i],
            recv_sem=recvs.at[i],
            device_id=peer,
            device_id_type=MESH,
        )

    pending = []

    def to_plane(stage, make):
        copies = []
        for d in range(1, PLANE):
            other, peer = plane_peer(d)
            source, target = make(d, other)
            c = copy(source, target, plane_send, plane_recv, stage * (PLANE - 1) + d - 1, peer)
            c.start()
            copies.append(c)
        pending.extend(copies)
        return copies

    def to_cubes(stage, source, target):
        copies = []
        for d in range(1, ZHI):
            c = copy(source, target, cube_send, cube_recv, stage * (ZHI - 1) + d - 1, cube_peer(d))
            c.start()
            copies.append(c)
        pending.extend(copies)
        return copies

    def to_grp(stage, source, target):
        copies = []
        for d in range(1, GRP):
            c = copy(source, target, grp_send, grp_recv, stage * (GRP - 1) + d - 1, grp_peer(d))
            c.start()
            copies.append(c)
        pending.extend(copies)
        return copies

    def arrived(copies):
        for c in copies:
            c.wait_recv()

    def summed(ref, count):
        out = ref[0]
        for j in range(1, count):
            out = out + ref[j]
        return out

    delta[...] = (scale / total) * jnp.dot(
        full.astype(jnp.bfloat16), data[:, pl.ds(start, share)], preferred_element_type=jnp.float32
    )

    pl.semaphore_wait(barrier, len(peers))

    def scatter(d, other):
        where = pl.ds(pl.multiple_of(other * piece, piece), piece)
        return delta.at[:, where], sums1.at[d - 1]

    scattered = to_plane(0, scatter)
    for j in range(PLANE):
        where = pl.ds(pl.multiple_of(start + j * piece, piece), piece)
        wide[j] = data[:, where].astype(jnp.float32)

    per_half = LANES // rows
    lane = lax.broadcasted_iota(jnp.int32, (1, LANES), 1) // rows
    known = jnp.concatenate([signs, visit.astype(jnp.float32), dual], axis=0)
    known = jnp.concatenate([known] * per_half, axis=1)
    known = jnp.where(lane == lax.rem(mine, per_half), known, 0.0)
    packed = jnp.concatenate([gram[8 * i : 8 * i + 8] for i in range(per_half)], axis=1)
    known = jnp.concatenate([packed, known], axis=0)
    facts_own[...] = known
    facts[mine] = known
    across[mine] = data[:, pl.ds(pl.multiple_of(start + mine * piece, piece), piece)].astype(
        jnp.float32
    )

    notes = to_plane(1, lambda d, other: (facts_own, facts.at[mine]))
    pieces = to_plane(2, lambda d, other: (wide.at[other], across.at[mine]))

    arrived(scattered)
    step = delta[:, own] + summed(sums1, PLANE - 1)

    held = None
    for r in range(ROUNDS):
        part2[r] = step
        sums2[r, zhi] = step
        cubes = to_cubes(r, part2.at[r], sums2.at[r, zhi])
        if r == 0:
            arrived(notes)
            half = PLANE // 2
            low_half, high_half = facts[0, 8:], facts[half, 8:]
            for j in range(1, half):
                low_half = low_half + facts[j, 8:]
                high_half = high_half + facts[half + j, 8:]
            known = jnp.concatenate([low_half, high_half], axis=1)
            signs, visit, dual = known[0:1], known[1:2].astype(jnp.int32), known[2:]
            gram = []
            for j in range(PLANE):
                packed = facts[j, :8]
                parts = [packed[:, i * rows : (i + 1) * rows] for i in range(per_half)]
                one = [jnp.concatenate(parts, axis=0)]
                if j:
                    one = [jnp.zeros((rows, j * rows), jnp.float32)] + one
                if j + 1 < PLANE:
                    one = one + [jnp.zeros((rows, (PLANE - 1 - j) * rows), jnp.float32)]
                gram.append(jnp.concatenate(one, axis=1))
            gram = jnp.concatenate(gram, axis=0)
            solve = local_round(gram, signs, visit)
            arrived(pieces)
            block = across[...].reshape(wide_rows, piece).astype(jnp.bfloat16)
        arrived(cubes)
        step = summed(sums2.at[r], ZHI)
        held = step if held is None else held + step

        tile = scale * lax.dot_general(
            held.astype(jnp.bfloat16), block, contract_last, preferred_element_type=jnp.float32
        )
        last = r + 1 == ROUNDS
        if last:
            norm = jnp.sum(held * held, axis=1, keepdims=True)
            lanes = lax.broadcasted_iota(jnp.int32, (REGS, wide_rows), 1)
            norm = jnp.sum(jnp.where(lanes == reg_row, norm, 0.0), axis=0, keepdims=True)
            tile = jnp.concatenate([tile, norm], axis=0)
        own3, all3, own4, all4 = (
            (last3, last_sums3, last4, last_sums4) if last else (local3, sums3, local4, sums4)
        )
        own3[...] = tile
        all3[mine] = tile
        arrived(to_plane(3 + r, lambda d, other: (own3, all3.at[mine])))
        tile = summed(all3, PLANE)
        own4[...] = tile
        all4[slot] = tile
        arrived(to_grp(r, own4, all4.at[slot]))
        tile = summed(all4, GRP)
        margins = tile[:REGS]
        if not last:
            full, dual = solve(margins, dual)
            step = (scale / total) * jnp.dot(
                full.astype(jnp.bfloat16), block, preferred_element_type=jnp.float32
            )

    hinge = jnp.maximum(0.0, 1.0 - signs * margins)
    cube_total = jnp.broadcast_to(jnp.sum(hinge - dual, axis=1, keepdims=True), (REGS, LANES))
    local5[...] = cube_total
    sums5[zhi] = cube_total
    cubes = to_cubes(ROUNDS, local5, sums5.at[zhi])

    chosen = reg_row == reg_ref[0]

    def own_rows(values):
        values = jnp.sum(jnp.where(chosen, values, 0.0), axis=0, keepdims=True)
        out = jnp.zeros((1, rows), jnp.float32)
        for j in range(PLANE):
            out = out + jnp.where(mine == j, values[:, j * rows : (j + 1) * rows], 0.0)
        return out

    own_dual, own_margins = own_rows(dual), own_rows(margins)
    norm = jnp.sum(
        jnp.where(lax.broadcasted_iota(jnp.int32, (1, wide_rows), 1) == reg_ref[0], tile[REGS:], 0.0),
        axis=1,
        keepdims=True,
    )
    arrived(cubes)
    everyone = summed(sums5, ZHI)[:, :1]
    gap = jnp.sum(jnp.where(chosen, everyone / samples_all, 0.0), axis=0, keepdims=True)
    gap = gap + norm * jnp.sum(jnp.where(chosen, strength, 0.0), axis=0, keepdims=True)
    rest = LANES - 2 * rows
    out[...] = jnp.concatenate([own_dual, own_margins, jnp.broadcast_to(gap, (1, rest))], axis=1)
    for c in pending:
        c.wait_send()


def handed_out(out, dual, margins, gap):
    rows = dual.shape[1]
    dual[...] = out[:, :rows]
    margins[...] = out[:, rows : 2 * rows]
    gap[...] = out[:, 2 * rows : 2 * rows + 1]


def shards(data, labels, order, reg_index):
    rows, features = data.shape
    share = features // GRP
    piece = share // PLANE
    chunks = 8
    f32 = functools.partial(jax.ShapeDtypeStruct, dtype=jnp.float32)
    vmem = pl.BlockSpec(memory_space=pltpu.VMEM)
    scratch = lambda *shape: pltpu.VMEM(shape, jnp.float32)
    sems = lambda n: pltpu.SemaphoreType.DMA((n,))
    wide_rows = PLANE * rows
    known = 8 + 2 + REGS
    out = pl.pallas_call(
        functools.partial(kernel, rows * lax.axis_size("blk"), chunks),
        out_shape=pltpu.VMEM((1, LANES), jnp.float32),
        in_specs=[pl.BlockSpec(memory_space=pl.ANY)] * 4,
        out_specs=vmem,
        scratch_shapes=[
            pltpu.VMEM((1, rows), jnp.int32),
            pltpu.SMEM((1, NBLOCKS), jnp.int32),
            pltpu.SMEM((1,), jnp.int32),
            sems(3),
            pltpu.VMEM((rows, features), jnp.bfloat16),
            sems(chunks),
            scratch(REGS, share),
            scratch(PLANE - 1, REGS, piece),
            scratch(ROUNDS, REGS, piece),
            scratch(ROUNDS, ZHI, REGS, piece),
            scratch(PLANE, rows, piece),
            scratch(PLANE, rows, piece),
            scratch(known, LANES),
            scratch(PLANE, known, LANES),
            scratch(REGS, wide_rows),
            scratch(PLANE, REGS, wide_rows),
            scratch(REGS, wide_rows),
            scratch(GRP, REGS, wide_rows),
            scratch(REGS + 1, wide_rows),
            scratch(PLANE, REGS + 1, wide_rows),
            scratch(REGS + 1, wide_rows),
            scratch(GRP, REGS + 1, wide_rows),
            scratch(REGS, LANES),
            scratch(ZHI, REGS, LANES),
            sems((3 + ROUNDS) * (PLANE - 1)),
            sems((3 + ROUNDS) * (PLANE - 1)),
            sems((ROUNDS + 1) * (ZHI - 1)),
            sems((ROUNDS + 1) * (ZHI - 1)),
            sems(ROUNDS * (GRP - 1)),
            sems(ROUNDS * (GRP - 1)),
        ],
        compiler_params=pltpu.CompilerParams(collective_id=0, has_side_effects=True),
    )(labels.reshape(1, rows), order, reg_index, data)
    return tuple(
        a.reshape(-1)
        for a in pl.pallas_call(
            handed_out,
            out_shape=(f32((1, rows)), f32((1, rows)), f32((1, 1))),
            in_specs=[vmem],
            out_specs=(vmem, vmem, vmem),
        )(pltpu.with_memory_space_constraint(out, pltpu.VMEM))
    )


def solution(mesh):
    placed = (P("blk", None), P("blk"), P("blk", None), P("grp"))
    return jax.shard_map(
        shards,
        mesh=mesh,
        in_specs=placed,
        out_specs=(P(("grp", "blk")), P(("grp", "blk")), P("grp")),
        check_vma=False,
    )
```

```python
import functools
import math

import jax
import jax.numpy as jnp
from jax import lax
from jax.experimental import pallas as pl
from jax.experimental.pallas import tpu as pltpu
from jax.sharding import PartitionSpec as P

NBLOCKS = 4
ROUNDS = 2
REGS = 6
Y, ZLO = 4, 4
X, ZHI, CORE = 4, 4, 2
PLANE = X * CORE
GRP = Y * ZLO
LANES = 128
MESH = pl.DeviceIdType.MESH


def kernel(
    samples_all,
    chunks,
    labels_hbm,
    order_hbm,
    reg_hbm,
    data_hbm,
    out,
    labels_ref,
    order_ref,
    reg_ref,
    small_sem,
    data,
    load_sem,
    delta,
    sums1,
    part2,
    sums2,
    wide,
    across,
    facts_own,
    facts,
    local3,
    sums3,
    local4,
    sums4,
    last3,
    last_sums3,
    last4,
    last_sums4,
    local5,
    sums5,
    plane_send,
    plane_recv,
    cube_send,
    cube_recv,
    grp_send,
    grp_recv,
):
    rows, features = data.shape
    width = features // chunks
    loads = [
        pltpu.make_async_copy(
            data_hbm.at[:, pl.ds(i * width, width)],
            data.at[:, pl.ds(i * width, width)],
            load_sem.at[i],
        )
        for i in range(chunks)
    ]
    for load in loads:
        load.start()
    small = [
        pltpu.make_async_copy(source, target, small_sem.at[i])
        for i, (source, target) in enumerate(
            [(labels_hbm, labels_ref), (order_hbm, order_ref), (reg_hbm, reg_ref)]
        )
    ]
    for load in small:
        load.start()
    share = features // GRP
    piece = share // PLANE
    wide_rows = PLANE * rows
    grp, blk = lax.axis_index("grp"), lax.axis_index("blk")
    y, zlo = grp // ZLO, lax.rem(grp, ZLO)
    x, zhi, core = blk // (ZHI * CORE), lax.rem(blk // CORE, ZHI), lax.rem(blk, CORE)
    part = lax.rem(zlo + 2 * (zhi // 2), ZLO)
    mine = x * CORE + core

    def plane_peer(d):
        other = lax.rem(mine + d, PLANE)
        return other, (grp, (other // CORE) * ZHI * CORE + zhi * CORE + lax.rem(other, CORE))

    def cube_peer(d):
        other = lax.rem(zhi + d, ZHI)
        other_zlo = lax.rem(part + 2 * (other // 2), ZLO)
        return (y * ZLO + other_zlo, x * ZHI * CORE + other * CORE + core)

    def grp_peer(d):
        return (lax.rem(grp + d, GRP), blk)

    peers = [cube_peer(d) for d in (2, 1, 3)]
    peers += [grp_peer(d) for d in range(1, GRP)]
    peers += [plane_peer(d)[1] for d in range(1, PLANE)]
    barrier = pltpu.get_barrier_semaphore()
    for peer in peers:
        pl.semaphore_signal(barrier, inc=1, device_id=peer, device_id_type=MESH)

    contract_last = (((1,), (1,)), ((), ()))
    gram = jnp.zeros((rows, rows), jnp.float32)
    for i, load in enumerate(loads):
        load.wait()
        block = data[:, pl.ds(i * width, width)]
        gram = gram + lax.dot_general(
            block, block, contract_last, preferred_element_type=jnp.float32
        )

    scale = 1.0 / math.sqrt(features)
    sigma = float(X * ZHI * CORE)
    reg_row = lax.broadcasted_iota(jnp.int32, (REGS, 1), 0)
    strength = 0.04 * jnp.exp(0.5 * math.log(2.0) * reg_row.astype(jnp.float32))
    total = strength * samples_all
    coupling = sigma * scale * scale / total

    def local_round(gram, signs, visit):
        n = gram.shape[0]
        row = lax.broadcasted_iota(jnp.int32, (n, n), 0)
        col = lax.broadcasted_iota(jnp.int32, (n, n), 1)
        diagonal = jnp.sum(jnp.where(row == col, gram, 0.0), axis=0, keepdims=True)
        gain = total / (sigma * (diagonal / features + 1e-6))
        high = gram.astype(jnp.bfloat16)
        low = (gram - high.astype(jnp.float32)).astype(jnp.bfloat16)

        def run(base, dual):
            full = jnp.zeros((REGS, n), jnp.float32)
            new_dual = dual
            for t in range(NBLOCKS):
                score = base
                if t:
                    coef = full.astype(jnp.bfloat16)
                    score = base + coupling * (
                        jnp.dot(coef, high, preferred_element_type=jnp.float32)
                        + jnp.dot(coef, low, preferred_element_type=jnp.float32)
                    )
                updated = jnp.clip(dual + gain * (1.0 - signs * score), 0.0, 1.0)
                step = (signs * (updated - dual)).astype(jnp.bfloat16).astype(jnp.float32)
                full = jnp.where(visit == t, step, full)
                new_dual = jnp.where(visit == t, updated, new_dual)
            return full, new_dual

        return run

    for load in small:
        load.wait()
    signs = labels_ref[...].astype(jnp.float32)
    block_of = lax.broadcasted_iota(jnp.int32, (1, rows), 1) // (rows // NBLOCKS)
    visit = jnp.zeros((1, rows), jnp.int32)
    for t in range(1, NBLOCKS):
        visit = jnp.where(block_of == order_ref[0, t], t, visit)
    zero = jnp.zeros((REGS, rows), jnp.float32)
    full, dual = local_round(gram, signs, visit)(zero, zero)

    slot = y * ZLO + part
    start = pl.multiple_of(slot * share, share)
    own = pl.ds(pl.multiple_of(mine * piece, piece), piece)

    def copy(source, target, sends, recvs, i, peer):
        return pltpu.make_async_remote_copy(
            src_ref=source,
            dst_ref=target,
            send_sem=sends.at[i],
            recv_sem=recvs.at[i],
            device_id=peer,
            device_id_type=MESH,
        )

    pending = []

    def to_plane(stage, make):
        copies = []
        for d in (4, 3, 5, 2, 6, 1, 7):
            other, peer = plane_peer(d)
            source, target = make(d, other)
            c = copy(source, target, plane_send, plane_recv, stage * (PLANE - 1) + d - 1, peer)
            c.start()
            copies.append(c)
        pending.extend(copies)
        return copies

    def to_cubes(stage, source, target):
        copies = []
        for d in (2, 1, 3):
            c = copy(source, target, cube_send, cube_recv, stage * (ZHI - 1) + d - 1, cube_peer(d))
            c.start()
            copies.append(c)
        pending.extend(copies)
        return copies

    def to_grp(stage, source, target):
        copies = []
        for d in (8, 7, 9, 6, 10, 5, 11, 4, 12, 3, 13, 2, 14, 1, 15):
            c = copy(source, target, grp_send, grp_recv, stage * (GRP - 1) + d - 1, grp_peer(d))
            c.start()
            copies.append(c)
        pending.extend(copies)
        return copies

    def arrived(copies):
        for c in copies:
            c.wait_recv()

    def summed(ref, count):
        out = ref[0]
        for j in range(1, count):
            out = out + ref[j]
        return out

    delta[...] = (scale / total) * jnp.dot(
        full.astype(jnp.bfloat16), data[:, pl.ds(start, share)], preferred_element_type=jnp.float32
    )

    pl.semaphore_wait(barrier, len(peers))

    def scatter(d, other):
        where = pl.ds(pl.multiple_of(other * piece, piece), piece)
        return delta.at[:, where], sums1.at[d - 1]

    scattered = to_plane(0, scatter)
    for j in range(PLANE):
        where = pl.ds(pl.multiple_of(start + j * piece, piece), piece)
        wide[j] = data[:, where].astype(jnp.float32)

    per_half = LANES // rows
    lane = lax.broadcasted_iota(jnp.int32, (1, LANES), 1) // rows
    known = jnp.concatenate([signs, visit.astype(jnp.float32), dual], axis=0)
    known = jnp.concatenate([known] * per_half, axis=1)
    known = jnp.where(lane == lax.rem(mine, per_half), known, 0.0)
    packed = jnp.concatenate([gram[8 * i : 8 * i + 8] for i in range(per_half)], axis=1)
    known = jnp.concatenate([packed, known], axis=0)
    facts_own[...] = known
    facts[mine] = known
    across[mine] = data[:, pl.ds(pl.multiple_of(start + mine * piece, piece), piece)].astype(
        jnp.float32
    )

    notes = to_plane(1, lambda d, other: (facts_own, facts.at[mine]))
    pieces = to_plane(2, lambda d, other: (wide.at[other], across.at[mine]))

    arrived(scattered)
    step = delta[:, own] + summed(sums1, PLANE - 1)

    held = None
    for r in range(ROUNDS):
        part2[r] = step
        sums2[r, zhi] = step
        cubes = to_cubes(r, part2.at[r], sums2.at[r, zhi])
        if r == 0:
            arrived(notes)
            half = PLANE // 2
            low_half, high_half = facts[0, 8:], facts[half, 8:]
            for j in range(1, half):
                low_half = low_half + facts[j, 8:]
                high_half = high_half + facts[half + j, 8:]
            known = jnp.concatenate([low_half, high_half], axis=1)
            signs, visit, dual = known[0:1], known[1:2].astype(jnp.int32), known[2:]
            gram = []
            for j in range(PLANE):
                packed = facts[j, :8]
                parts = [packed[:, i * rows : (i + 1) * rows] for i in range(per_half)]
                one = [jnp.concatenate(parts, axis=0)]
                if j:
                    one = [jnp.zeros((rows, j * rows), jnp.float32)] + one
                if j + 1 < PLANE:
                    one = one + [jnp.zeros((rows, (PLANE - 1 - j) * rows), jnp.float32)]
                gram.append(jnp.concatenate(one, axis=1))
            gram = jnp.concatenate(gram, axis=0)
            solve = local_round(gram, signs, visit)
            arrived(pieces)
            block = across[...].reshape(wide_rows, piece).astype(jnp.bfloat16)
        arrived(cubes)
        step = summed(sums2.at[r], ZHI)
        held = step if held is None else held + step

        tile = scale * lax.dot_general(
            held.astype(jnp.bfloat16), block, contract_last, preferred_element_type=jnp.float32
        )
        last = r + 1 == ROUNDS
        if last:
            norm = jnp.sum(held * held, axis=1, keepdims=True)
            lanes = lax.broadcasted_iota(jnp.int32, (REGS, wide_rows), 1)
            norm = jnp.sum(jnp.where(lanes == reg_row, norm, 0.0), axis=0, keepdims=True)
            tile = jnp.concatenate([tile, norm], axis=0)
        own3, all3, own4, all4 = (
            (last3, last_sums3, last4, last_sums4) if last else (local3, sums3, local4, sums4)
        )
        own3[...] = tile
        all3[mine] = tile
        arrived(to_plane(3 + r, lambda d, other: (own3, all3.at[mine])))
        tile = summed(all3, PLANE)
        own4[...] = tile
        all4[slot] = tile
        arrived(to_grp(r, own4, all4.at[slot]))
        tile = summed(all4, GRP)
        margins = tile[:REGS]
        if not last:
            full, dual = solve(margins, dual)
            step = (scale / total) * jnp.dot(
                full.astype(jnp.bfloat16), block, preferred_element_type=jnp.float32
            )

    hinge = jnp.maximum(0.0, 1.0 - signs * margins)
    cube_total = jnp.broadcast_to(jnp.sum(hinge - dual, axis=1, keepdims=True), (REGS, LANES))
    local5[...] = cube_total
    sums5[zhi] = cube_total
    cubes = to_cubes(ROUNDS, local5, sums5.at[zhi])

    chosen = reg_row == reg_ref[0]

    def own_rows(values):
        values = jnp.sum(jnp.where(chosen, values, 0.0), axis=0, keepdims=True)
        out = jnp.zeros((1, rows), jnp.float32)
        for j in range(PLANE):
            out = out + jnp.where(mine == j, values[:, j * rows : (j + 1) * rows], 0.0)
        return out

    own_dual, own_margins = own_rows(dual), own_rows(margins)
    norm = jnp.sum(
        jnp.where(lax.broadcasted_iota(jnp.int32, (1, wide_rows), 1) == reg_ref[0], tile[REGS:], 0.0),
        axis=1,
        keepdims=True,
    )
    arrived(cubes)
    everyone = summed(sums5, ZHI)[:, :1]
    gap = jnp.sum(jnp.where(chosen, everyone / samples_all, 0.0), axis=0, keepdims=True)
    gap = gap + norm * jnp.sum(jnp.where(chosen, strength, 0.0), axis=0, keepdims=True)
    rest = LANES - 2 * rows
    out[...] = jnp.concatenate([own_dual, own_margins, jnp.broadcast_to(gap, (1, rest))], axis=1)
    for c in pending:
        c.wait_send()


def handed_out(out, dual, margins, gap):
    rows = dual.shape[1]
    dual[...] = out[:, :rows]
    margins[...] = out[:, rows : 2 * rows]
    gap[...] = out[:, 2 * rows : 2 * rows + 1]


def shards(data, labels, order, reg_index):
    rows, features = data.shape
    share = features // GRP
    piece = share // PLANE
    chunks = 8
    f32 = functools.partial(jax.ShapeDtypeStruct, dtype=jnp.float32)
    vmem = pl.BlockSpec(memory_space=pltpu.VMEM)
    scratch = lambda *shape: pltpu.VMEM(shape, jnp.float32)
    sems = lambda n: pltpu.SemaphoreType.DMA((n,))
    wide_rows = PLANE * rows
    known = 8 + 2 + REGS
    out = pl.pallas_call(
        functools.partial(kernel, rows * lax.axis_size("blk"), chunks),
        out_shape=pltpu.VMEM((1, LANES), jnp.float32),
        in_specs=[pl.BlockSpec(memory_space=pl.ANY)] * 4,
        out_specs=vmem,
        scratch_shapes=[
            pltpu.VMEM((1, rows), jnp.int32),
            pltpu.SMEM((1, NBLOCKS), jnp.int32),
            pltpu.SMEM((1,), jnp.int32),
            sems(3),
            pltpu.VMEM((rows, features), jnp.bfloat16),
            sems(chunks),
            scratch(REGS, share),
            scratch(PLANE - 1, REGS, piece),
            scratch(ROUNDS, REGS, piece),
            scratch(ROUNDS, ZHI, REGS, piece),
            scratch(PLANE, rows, piece),
            scratch(PLANE, rows, piece),
            scratch(known, LANES),
            scratch(PLANE, known, LANES),
            scratch(REGS, wide_rows),
            scratch(PLANE, REGS, wide_rows),
            scratch(REGS, wide_rows),
            scratch(GRP, REGS, wide_rows),
            scratch(REGS + 1, wide_rows),
            scratch(PLANE, REGS + 1, wide_rows),
            scratch(REGS + 1, wide_rows),
            scratch(GRP, REGS + 1, wide_rows),
            scratch(REGS, LANES),
            scratch(ZHI, REGS, LANES),
            sems((3 + ROUNDS) * (PLANE - 1)),
            sems((3 + ROUNDS) * (PLANE - 1)),
            sems((ROUNDS + 1) * (ZHI - 1)),
            sems((ROUNDS + 1) * (ZHI - 1)),
            sems(ROUNDS * (GRP - 1)),
            sems(ROUNDS * (GRP - 1)),
        ],
        compiler_params=pltpu.CompilerParams(collective_id=0, has_side_effects=True),
    )(labels.reshape(1, rows), order, reg_index, data)
    return tuple(
        a.reshape(-1)
        for a in pl.pallas_call(
            handed_out,
            out_shape=(f32((1, rows)), f32((1, rows)), f32((1, 1))),
            in_specs=[vmem],
            out_specs=(vmem, vmem, vmem),
        )(pltpu.with_memory_space_constraint(out, pltpu.VMEM))
    )


def solution(mesh):
    placed = (P("blk", None), P("blk"), P("blk", None), P("grp"))
    return jax.shard_map(
        shards,
        mesh=mesh,
        in_specs=placed,
        out_specs=(P(("grp", "blk")), P(("grp", "blk")), P("grp")),
        check_vma=False,
    )
```

```python
import functools
import math

import jax
import jax.numpy as jnp
from jax import lax
from jax.experimental import pallas as pl
from jax.experimental.pallas import tpu as pltpu
from jax.sharding import PartitionSpec as P

NBLOCKS = 4
ROUNDS = 2
REGS = 6
Y, ZLO = 4, 4
X, ZHI, CORE = 4, 4, 2
PLANE = X * CORE
GRP = Y * ZLO
LANES = 128
MESH = pl.DeviceIdType.MESH


def kernel(
    samples_all,
    chunks,
    labels_hbm,
    order_hbm,
    reg_hbm,
    data_hbm,
    out,
    labels_ref,
    order_ref,
    reg_ref,
    small_sem,
    data,
    load_sem,
    delta,
    sums1,
    part2,
    sums2,
    wide,
    across,
    facts_own,
    facts,
    local3,
    sums3,
    local4,
    sums4,
    last3,
    last_sums3,
    last4,
    last_sums4,
    local5,
    sums5,
    plane_send,
    plane_recv,
    cube_send,
    cube_recv,
    grp_send,
    grp_recv,
):
    rows, features = data.shape
    width = features // chunks
    loads = [
        pltpu.make_async_copy(
            data_hbm.at[:, pl.ds(i * width, width)],
            data.at[:, pl.ds(i * width, width)],
            load_sem.at[i],
        )
        for i in range(chunks)
    ]
    for load in loads:
        load.start()
    small = [
        pltpu.make_async_copy(source, target, small_sem.at[i])
        for i, (source, target) in enumerate(
            [(labels_hbm, labels_ref), (order_hbm, order_ref), (reg_hbm, reg_ref)]
        )
    ]
    for load in small:
        load.start()
    share = features // GRP
    piece = share // PLANE
    wide_rows = PLANE * rows
    grp, blk = lax.axis_index("grp"), lax.axis_index("blk")
    y, zlo = grp // ZLO, lax.rem(grp, ZLO)
    x, zhi, core = blk // (ZHI * CORE), lax.rem(blk // CORE, ZHI), lax.rem(blk, CORE)
    part = lax.rem(zlo + 2 * (zhi // 2), ZLO)
    mine = x * CORE + core

    def plane_peer(d):
        other = lax.rem(mine + d, PLANE)
        return other, (grp, (other // CORE) * ZHI * CORE + zhi * CORE + lax.rem(other, CORE))

    def cube_peer(d):
        other = lax.rem(zhi + d, ZHI)
        other_zlo = lax.rem(part + 2 * (other // 2), ZLO)
        return (y * ZLO + other_zlo, x * ZHI * CORE + other * CORE + core)

    def grp_peer(d):
        return (lax.rem(grp + d, GRP), blk)

    peers = [cube_peer(d) for d in (2, 1, 3)]
    peers += [grp_peer(d) for d in range(1, GRP)]
    peers += [plane_peer(d)[1] for d in range(1, PLANE)]
    barrier = pltpu.get_barrier_semaphore()
    for peer in peers:
        pl.semaphore_signal(barrier, inc=1, device_id=peer, device_id_type=MESH)

    contract_last = (((1,), (1,)), ((), ()))
    gram = jnp.zeros((rows, rows), jnp.float32)
    for i, load in enumerate(loads):
        load.wait()
        block = data[:, pl.ds(i * width, width)]
        gram = gram + lax.dot_general(
            block, block, contract_last, preferred_element_type=jnp.float32
        )

    scale = 1.0 / math.sqrt(features)
    sigma = float(X * ZHI * CORE)
    reg_row = lax.broadcasted_iota(jnp.int32, (REGS, 1), 0)
    strength = 0.04 * jnp.exp(0.5 * math.log(2.0) * reg_row.astype(jnp.float32))
    total = strength * samples_all
    coupling = sigma * scale * scale / total

    def local_round(gram, signs, visit):
        n = gram.shape[0]
        row = lax.broadcasted_iota(jnp.int32, (n, n), 0)
        col = lax.broadcasted_iota(jnp.int32, (n, n), 1)
        diagonal = jnp.sum(jnp.where(row == col, gram, 0.0), axis=0, keepdims=True)
        gain = total / (sigma * (diagonal / features + 1e-6))
        high = gram.astype(jnp.bfloat16)
        low = (gram - high.astype(jnp.float32)).astype(jnp.bfloat16)

        def run(base, dual):
            full = jnp.zeros((REGS, n), jnp.float32)
            new_dual = dual
            for t in range(NBLOCKS):
                score = base
                if t:
                    coef = full.astype(jnp.bfloat16)
                    score = base + coupling * (
                        jnp.dot(coef, high, preferred_element_type=jnp.float32)
                        + jnp.dot(coef, low, preferred_element_type=jnp.float32)
                    )
                updated = jnp.clip(dual + gain * (1.0 - signs * score), 0.0, 1.0)
                step = (signs * (updated - dual)).astype(jnp.bfloat16).astype(jnp.float32)
                full = jnp.where(visit == t, step, full)
                new_dual = jnp.where(visit == t, updated, new_dual)
            return full, new_dual

        return run

    for load in small:
        load.wait()
    signs = labels_ref[...].astype(jnp.float32)
    block_of = lax.broadcasted_iota(jnp.int32, (1, rows), 1) // (rows // NBLOCKS)
    visit = jnp.zeros((1, rows), jnp.int32)
    for t in range(1, NBLOCKS):
        visit = jnp.where(block_of == order_ref[0, t], t, visit)
    zero = jnp.zeros((REGS, rows), jnp.float32)
    full, dual = local_round(gram, signs, visit)(zero, zero)

    slot = y * ZLO + part
    start = pl.multiple_of(slot * share, share)
    own = pl.ds(pl.multiple_of(mine * piece, piece), piece)

    def copy(source, target, sends, recvs, i, peer):
        return pltpu.make_async_remote_copy(
            src_ref=source,
            dst_ref=target,
            send_sem=sends.at[i],
            recv_sem=recvs.at[i],
            device_id=peer,
            device_id_type=MESH,
        )

    pending = []

    def to_plane(stage, make):
        copies = []
        for d in (4, 3, 5, 2, 6, 1, 7):
            other, peer = plane_peer(d)
            source, target = make(d, other)
            c = copy(source, target, plane_send, plane_recv, stage * (PLANE - 1) + d - 1, peer)
            c.start()
            copies.append(c)
        pending.extend(copies)
        return copies

    def to_cubes(stage, source, target):
        copies = []
        for d in (2, 1, 3):
            c = copy(source, target, cube_send, cube_recv, stage * (ZHI - 1) + d - 1, cube_peer(d))
            c.start()
            copies.append(c)
        pending.extend(copies)
        return copies

    def to_grp(stage, source, target):
        copies = []
        for d in (8, 7, 9, 6, 10, 5, 11, 4, 12, 3, 13, 2, 14, 1, 15):
            c = copy(source, target, grp_send, grp_recv, stage * (GRP - 1) + d - 1, grp_peer(d))
            c.start()
            copies.append(c)
        pending.extend(copies)
        return copies

    def arrived(copies):
        for c in copies:
            c.wait_recv()

    def summed(ref, count):
        out = ref[0]
        for j in range(1, count):
            out = out + ref[j]
        return out

    delta[...] = (scale / total) * jnp.dot(
        full.astype(jnp.bfloat16), data[:, pl.ds(start, share)], preferred_element_type=jnp.float32
    )

    pl.semaphore_wait(barrier, len(peers))

    def scatter(d, other):
        where = pl.ds(pl.multiple_of(other * piece, piece), piece)
        return delta.at[:, where], sums1.at[d - 1]

    scattered = to_plane(0, scatter)
    for j in range(PLANE):
        where = pl.ds(pl.multiple_of(start + j * piece, piece), piece)
        wide[j] = data[:, where].astype(jnp.float32)

    per_half = LANES // rows
    lane = lax.broadcasted_iota(jnp.int32, (1, LANES), 1) // rows
    known = jnp.concatenate([signs, visit.astype(jnp.float32), dual], axis=0)
    known = jnp.concatenate([known] * per_half, axis=1)
    known = jnp.where(lane == lax.rem(mine, per_half), known, 0.0)
    packed = jnp.concatenate([gram[8 * i : 8 * i + 8] for i in range(per_half)], axis=1)
    known = jnp.concatenate([packed, known], axis=0)
    facts_own[...] = known
    facts[mine] = known
    across[mine] = data[:, pl.ds(pl.multiple_of(start + mine * piece, piece), piece)].astype(
        jnp.float32
    )

    notes = to_plane(1, lambda d, other: (facts_own, facts.at[mine]))

    arrived(scattered)
    step = delta[:, own] + summed(sums1, PLANE - 1)

    held = None
    for r in range(ROUNDS):
        part2[r] = step
        sums2[r, zhi] = step
        cubes = to_cubes(r, part2.at[r], sums2.at[r, zhi])
        if r == 0:
            pieces = to_plane(2, lambda d, other: (wide.at[other], across.at[mine]))
            arrived(notes)
            half = PLANE // 2
            low_half, high_half = facts[0, 8:], facts[half, 8:]
            for j in range(1, half):
                low_half = low_half + facts[j, 8:]
                high_half = high_half + facts[half + j, 8:]
            known = jnp.concatenate([low_half, high_half], axis=1)
            signs, visit, dual = known[0:1], known[1:2].astype(jnp.int32), known[2:]
            gram = []
            for j in range(PLANE):
                packed = facts[j, :8]
                parts = [packed[:, i * rows : (i + 1) * rows] for i in range(per_half)]
                one = [jnp.concatenate(parts, axis=0)]
                if j:
                    one = [jnp.zeros((rows, j * rows), jnp.float32)] + one
                if j + 1 < PLANE:
                    one = one + [jnp.zeros((rows, (PLANE - 1 - j) * rows), jnp.float32)]
                gram.append(jnp.concatenate(one, axis=1))
            gram = jnp.concatenate(gram, axis=0)
            solve = local_round(gram, signs, visit)
            arrived(pieces)
            block = across[...].reshape(wide_rows, piece).astype(jnp.bfloat16)
        arrived(cubes)
        step = summed(sums2.at[r], ZHI)
        held = step if held is None else held + step

        tile = scale * lax.dot_general(
            held.astype(jnp.bfloat16), block, contract_last, preferred_element_type=jnp.float32
        )
        last = r + 1 == ROUNDS
        if last:
            norm = jnp.sum(held * held, axis=1, keepdims=True)
            lanes = lax.broadcasted_iota(jnp.int32, (REGS, wide_rows), 1)
            norm = jnp.sum(jnp.where(lanes == reg_row, norm, 0.0), axis=0, keepdims=True)
            tile = jnp.concatenate([tile, norm], axis=0)
        own3, all3, own4, all4 = (
            (last3, last_sums3, last4, last_sums4) if last else (local3, sums3, local4, sums4)
        )
        own3[...] = tile
        all3[mine] = tile
        arrived(to_plane(3 + r, lambda d, other: (own3, all3.at[mine])))
        tile = summed(all3, PLANE)
        own4[...] = tile
        all4[slot] = tile
        arrived(to_grp(r, own4, all4.at[slot]))
        tile = summed(all4, GRP)
        margins = tile[:REGS]
        if not last:
            full, dual = solve(margins, dual)
            step = (scale / total) * jnp.dot(
                full.astype(jnp.bfloat16), block, preferred_element_type=jnp.float32
            )

    hinge = jnp.maximum(0.0, 1.0 - signs * margins)
    cube_total = jnp.broadcast_to(jnp.sum(hinge - dual, axis=1, keepdims=True), (REGS, LANES))
    local5[...] = cube_total
    sums5[zhi] = cube_total
    cubes = to_cubes(ROUNDS, local5, sums5.at[zhi])

    chosen = reg_row == reg_ref[0]

    def own_rows(values):
        values = jnp.sum(jnp.where(chosen, values, 0.0), axis=0, keepdims=True)
        out = jnp.zeros((1, rows), jnp.float32)
        for j in range(PLANE):
            out = out + jnp.where(mine == j, values[:, j * rows : (j + 1) * rows], 0.0)
        return out

    own_dual, own_margins = own_rows(dual), own_rows(margins)
    norm = jnp.sum(
        jnp.where(lax.broadcasted_iota(jnp.int32, (1, wide_rows), 1) == reg_ref[0], tile[REGS:], 0.0),
        axis=1,
        keepdims=True,
    )
    arrived(cubes)
    everyone = summed(sums5, ZHI)[:, :1]
    gap = jnp.sum(jnp.where(chosen, everyone / samples_all, 0.0), axis=0, keepdims=True)
    gap = gap + norm * jnp.sum(jnp.where(chosen, strength, 0.0), axis=0, keepdims=True)
    rest = LANES - 2 * rows
    out[...] = jnp.concatenate([own_dual, own_margins, jnp.broadcast_to(gap, (1, rest))], axis=1)
    for c in pending:
        c.wait_send()


def handed_out(out, dual, margins, gap):
    rows = dual.shape[1]
    dual[...] = out[:, :rows]
    margins[...] = out[:, rows : 2 * rows]
    gap[...] = out[:, 2 * rows : 2 * rows + 1]


def shards(data, labels, order, reg_index):
    rows, features = data.shape
    share = features // GRP
    piece = share // PLANE
    chunks = 8
    f32 = functools.partial(jax.ShapeDtypeStruct, dtype=jnp.float32)
    vmem = pl.BlockSpec(memory_space=pltpu.VMEM)
    scratch = lambda *shape: pltpu.VMEM(shape, jnp.float32)
    sems = lambda n: pltpu.SemaphoreType.DMA((n,))
    wide_rows = PLANE * rows
    known = 8 + 2 + REGS
    out = pl.pallas_call(
        functools.partial(kernel, rows * lax.axis_size("blk"), chunks),
        out_shape=pltpu.VMEM((1, LANES), jnp.float32),
        in_specs=[pl.BlockSpec(memory_space=pl.ANY)] * 4,
        out_specs=vmem,
        scratch_shapes=[
            pltpu.VMEM((1, rows), jnp.int32),
            pltpu.SMEM((1, NBLOCKS), jnp.int32),
            pltpu.SMEM((1,), jnp.int32),
            sems(3),
            pltpu.VMEM((rows, features), jnp.bfloat16),
            sems(chunks),
            scratch(REGS, share),
            scratch(PLANE - 1, REGS, piece),
            scratch(ROUNDS, REGS, piece),
            scratch(ROUNDS, ZHI, REGS, piece),
            scratch(PLANE, rows, piece),
            scratch(PLANE, rows, piece),
            scratch(known, LANES),
            scratch(PLANE, known, LANES),
            scratch(REGS, wide_rows),
            scratch(PLANE, REGS, wide_rows),
            scratch(REGS, wide_rows),
            scratch(GRP, REGS, wide_rows),
            scratch(REGS + 1, wide_rows),
            scratch(PLANE, REGS + 1, wide_rows),
            scratch(REGS + 1, wide_rows),
            scratch(GRP, REGS + 1, wide_rows),
            scratch(REGS, LANES),
            scratch(ZHI, REGS, LANES),
            sems((3 + ROUNDS) * (PLANE - 1)),
            sems((3 + ROUNDS) * (PLANE - 1)),
            sems((ROUNDS + 1) * (ZHI - 1)),
            sems((ROUNDS + 1) * (ZHI - 1)),
            sems(ROUNDS * (GRP - 1)),
            sems(ROUNDS * (GRP - 1)),
        ],
        compiler_params=pltpu.CompilerParams(collective_id=0, has_side_effects=True),
    )(labels.reshape(1, rows), order, reg_index, data)
    return tuple(
        a.reshape(-1)
        for a in pl.pallas_call(
            handed_out,
            out_shape=(f32((1, rows)), f32((1, rows)), f32((1, 1))),
            in_specs=[vmem],
            out_specs=(vmem, vmem, vmem),
        )(pltpu.with_memory_space_constraint(out, pltpu.VMEM))
    )


def solution(mesh):
    placed = (P("blk", None), P("blk"), P("blk", None), P("grp"))
    return jax.shard_map(
        shards,
        mesh=mesh,
        in_specs=placed,
        out_specs=(P(("grp", "blk")), P(("grp", "blk")), P("grp")),
        check_vma=False,
    )
```
